512 devices in a mesh: segment: 4 (over x), shard: 128 (over z, y, core).
Axes of the slice: x: 4, y: 8, z: 8, core: 2. Of those that a mesh axis runs over, the one named last changes fastest.
Arguments:
- proposal_attributes: bfloat16 [2, 65536, 1024], P(None, 'shard'), may hold values from -6 to 6
- keeper_ordering_vectors: bfloat16 [2, 16384, 4096], P(None, 'shard'), may hold values from -6 to 6
- keeper_positions: int32 [2, 16384], P(None, 'shard'), may hold values from 0 to 511
- alive_tallies: int32 [2, 128], P(None, 'shard'), may hold values from 256 to 512
- holder_shards: int32 [2, 16384, 1], P(None, 'shard'), may hold values from 0 to 127; in each aligned block of 128 rows (0 to 127, 128 to 255, ..., all dimensions but the last counted through in order) at most 2 rows name the same one
- holder_attribute_factor: bfloat16 [128, 4096], P('shard'), may hold values from 0.099609375 to 1.8984375
- early_inner_matrix: bfloat16 [1024, 1024], replicated, may hold values from -0.1875 to 0.1875
- early_inner_offset: float32 [1024], replicated, may hold values from -3 to 3
- early_grading_vector: bfloat16 [1024], replicated, may hold values from -0.1875 to 0.1875
- block_lowering_matrices: bfloat16 [3, 4096, 128], P(None, 'shard'), may hold values from -0.09375 to 0.09375
- block_raising_flipped: bfloat16 [3, 4096, 128], P(None, 'shard'), may hold values from -0.5 to 0.5
- block_result_offsets: float32 [3, 4096], replicated, may hold values from -3 to 3
- block_grading_vectors: float32 [3, 4096], replicated, may hold values from -0.09375 to 0.09375
Outputs:
- exits: float32 [4, 2, 32768], P('segment', None, 'shard')
The draws below stay inside these ranges and needn't reach their ends.
Inputs may be any that keep to these rules, and one draw needn't show every extreme that they name: `holder_shards`: in every round at most 2 entries of one block of 128 go to one owner. `keeper_positions`: entries at or above the block's count in alive_tallies are padding.
All inputs are finite; a program needn't handle non-finite values.
Results may differ from the reference program's by a relative error of at most 0.02.
Values may be sent and summed in bfloat16 or wider, within the bound.
A program may use at most 64 MiB of HBM per device.

```python
import math
import jax
import jax.numpy as jnp
import numpy as np
from jax import lax

D_PRE = 1024
ORDERING_WIDTH = 4096
LOW_RANK = 128
QUERY_PASSES = 2
PROPOSAL_TOTAL = 512
KEEPER_TOTAL = 128
SLOT_LIMIT = 2
PLACE_TOTAL = 256
N_SHARD = 128


def touch_ends(array, key, least, high):
    dims = array.shape
    place = [jax.random.randint(jax.random.fold_in(key, axis), (), 0, dims[axis]) for axis in range(len(dims))]
    array = array.at[tuple(place)].set(least)
    longest = dims.index(max(dims))
    place[longest] = (place[longest] + 1) % dims[longest]
    return array.at[tuple(place)].set(high)


def steps_of(key, dims, shards, low, top_value):
    level = 1.0
    for position, blocks in shards:
        draws = jax.random.uniform(jax.random.fold_in(jax.random.fold_in(key, 6), position), (blocks,), jnp.float32, low / len(shards), top_value / len(shards))
        level = level * jnp.repeat(jnp.exp(draws), dims[position] // blocks).reshape((-1,) + (1,) * (len(dims) - 1 - position))
    return level


def deal_out(key, own, number, rows, count, top, bound, lean):
    sequence = jax.random.permutation(key, count)
    heavy_load, usual = portions_of(count, rows * top, bound, lean, True), portions_of(count, rows * top, bound, lean, False)
    places = jnp.arange(count)

    def named(lengths, turn):
        used = int((lengths > 0).sum())
        fixed = max(1, used // 4)
        shifted = fixed + (places - fixed + turn * (used - fixed)) % max(1, count - fixed)
        return jnp.zeros((count,), jnp.int32).at[sequence[jnp.where(places < fixed, places, shifted)]].set(jnp.asarray(lengths, jnp.int32))

    lengths = jnp.where(number % 4 == 0, named(heavy_load, number // 4), named(usual, number - number // 4 - 1))
    mixed = jax.random.permutation(jax.random.fold_in(own, 3), count)
    donor, taker = mixed[0:count // 2 * 2:2], mixed[1:count // 2 * 2:2]
    room = jnp.minimum(lengths[donor] - 1, bound - lengths[taker]) // 2
    room = jnp.where((donor == sequence[0]) | (taker == sequence[0]) | (lengths[taker] == 0), 0, jnp.maximum(room, 0))
    shifted = jax.random.randint(jax.random.fold_in(own, 4), (count // 2,), 0, 1 << 20) % (room + 1)
    lengths = lengths.at[donor].add(-shifted).at[taker].add(shifted)
    labels = jnp.searchsorted(jnp.cumsum(lengths), jnp.arange(rows * top), side="right").astype(jnp.int32)
    grid = labels.reshape(top, rows).T
    grid = grid[jax.random.permutation(jax.random.fold_in(own, 1), rows)]
    turn = jax.random.randint(jax.random.fold_in(own, 2), (rows, 1), 0, top)
    return jnp.take_along_axis(grid, (jnp.arange(top)[None, :] + turn) % top, axis=1)


def portions_of(count, total, limit, slope, full):
    loads = [(1 << 20) // math.isqrt(standing ** slope) + 1 for standing in range(1, count + 1)]
    largest = limit if full else min(limit, max(-(-total // count), total * loads[0] // sum(loads)))
    least = 1 if total - largest >= count - 1 else 0
    counts, surplus = [largest] + [least] * (count - 1), total - largest - least * (count - 1)
    while surplus > 0:
        free = [i for i in range(1, count) if counts[i] < largest] or [i for i in range(1, count) if counts[i] < limit]
        whole, budget = sum([loads[i] for i in free]), surplus
        for i in free:
            more = min(limit - counts[i], max(1, budget * loads[i] // whole), surplus)
            counts[i] = counts[i] + more
            surplus = surplus - more
    return np.array(counts)


def scatter_about(rng, shape, width, reach, shards=(), kind=jnp.bfloat16):
    array = width * jax.random.normal(rng, shape, jnp.float32)
    if shards:
        array = array * steps_of(rng, shape, shards, -0.22, 0.18)
    return jnp.clip(array, -reach, reach).astype(kind)


def setup_inputs(seed: int = 0) -> dict:
    key_list = jax.random.split(jax.random.key(seed), 14)
    proposal_attributes = scatter_about(key_list[0], (QUERY_PASSES, N_SHARD * PROPOSAL_TOTAL, D_PRE), 1.0, 6.0, ((1, 128),))
    keeper_ordering_vectors = scatter_about(key_list[1], (QUERY_PASSES, N_SHARD * KEEPER_TOTAL, ORDERING_WIDTH), 1.0, 6.0, ((1, 128),))
    keeper_positions = touch_ends(jax.random.randint(key_list[2], (QUERY_PASSES, N_SHARD * KEEPER_TOTAL), 0, PROPOSAL_TOTAL), jax.random.fold_in(key_list[2], 1), 0, PROPOSAL_TOTAL - 1).astype(jnp.int32)
    alive_tallies = touch_ends(jax.random.randint(key_list[3], (QUERY_PASSES, N_SHARD), PROPOSAL_TOTAL // 2, PROPOSAL_TOTAL + 1), jax.random.fold_in(key_list[3], 1), PROPOSAL_TOTAL // 2, PROPOSAL_TOTAL).astype(jnp.int32)
    holder_shards_keys = jax.random.split(jax.random.fold_in(key_list[4], 1), QUERY_PASSES * (N_SHARD * KEEPER_TOTAL) // KEEPER_TOTAL)
    holder_shards_turns = jax.random.permutation(jax.random.fold_in(key_list[4], 3), QUERY_PASSES * (N_SHARD * KEEPER_TOTAL) // KEEPER_TOTAL)
    holder_shards = jax.vmap(lambda own, number: deal_out(jax.random.fold_in(key_list[4], 2), own, number, KEEPER_TOTAL, N_SHARD, 1, SLOT_LIMIT, 2))(holder_shards_keys, holder_shards_turns).reshape((QUERY_PASSES, N_SHARD * KEEPER_TOTAL, 1))
    holder_attribute_factor = jnp.clip(1.0 + 0.18 * jax.random.normal(key_list[5], (N_SHARD, ORDERING_WIDTH), jnp.float32), 0.099609375, 1.8984375).astype(jnp.bfloat16)
    early_inner_matrix = scatter_about(key_list[6], (D_PRE, D_PRE), D_PRE ** -0.5, 0.1875)
    early_inner_offset = scatter_about(key_list[7], (D_PRE,), 0.5, 3.0, (), jnp.float32)
    early_grading_vector = scatter_about(key_list[8], (D_PRE,), D_PRE ** -0.5, 0.1875)
    block_lowering_matrices = scatter_about(key_list[9], (3, ORDERING_WIDTH, LOW_RANK), ORDERING_WIDTH ** -0.5, 0.09375, ((1, 128),))
    block_raising_flipped = scatter_about(key_list[10], (3, ORDERING_WIDTH, LOW_RANK), LOW_RANK ** -0.5, 0.5, ((1, 128),))
    block_result_offsets = scatter_about(key_list[11], (3, ORDERING_WIDTH), 0.5, 3.0, (), jnp.float32)
    block_grading_vectors = scatter_about(key_list[12], (3, ORDERING_WIDTH), ORDERING_WIDTH ** -0.5, 0.09375, (), jnp.float32)
    return dict(proposal_attributes=proposal_attributes, keeper_ordering_vectors=keeper_ordering_vectors, keeper_positions=keeper_positions, alive_tallies=alive_tallies, holder_shards=holder_shards, holder_attribute_factor=holder_attribute_factor, early_inner_matrix=early_inner_matrix, early_inner_offset=early_inner_offset, early_grading_vector=early_grading_vector, block_lowering_matrices=block_lowering_matrices, block_raising_flipped=block_raising_flipped, block_result_offsets=block_result_offsets, block_grading_vectors=block_grading_vectors)


def rank_section(row_block, flag_vals, gain_rows, up_weight, back_weight, bias_vec, head_vec, crossing):
    if crossing:
        row_block = (row_block.astype(jnp.float32) * gain_rows).astype(jnp.bfloat16)
    inner_proj = jnp.dot(row_block, up_weight, preferred_element_type=jnp.float32)
    active = jnp.where(crossing, inner_proj, jax.nn.relu(inner_proj)).astype(jnp.bfloat16)
    lifted = lax.dot_general(active, back_weight, (((1,), (1,)), ((), ())), preferred_element_type=jnp.float32) + bias_vec
    base_rows = row_block.astype(jnp.float32)
    result = (base_rows + jnp.where(crossing, base_rows * lifted, lifted)) * flag_vals[:, None]
    raw_activations = jnp.sum(result * head_vec, axis=1)
    return result.astype(jnp.bfloat16), raw_activations


def reference(proposal_attributes, keeper_ordering_vectors, keeper_positions, alive_tallies, holder_shards, holder_attribute_factor, early_inner_matrix, early_inner_offset, early_grading_vector, block_lowering_matrices, block_raising_flipped, block_result_offsets, block_grading_vectors):
    sender_labels = jnp.broadcast_to(jnp.arange(N_SHARD, dtype=jnp.int32)[:, None], (N_SHARD, KEEPER_TOTAL))
    columns = jnp.arange(N_SHARD, dtype=jnp.int32)
    segment_lists = [[], [], [], []]
    for query_pass_number in range(QUERY_PASSES):
        hidden = jax.nn.relu(jnp.dot(proposal_attributes[query_pass_number], early_inner_matrix, preferred_element_type=jnp.float32) + early_inner_offset).astype(jnp.bfloat16)
        scores = jnp.dot(hidden, early_grading_vector, preferred_element_type=jnp.float32).reshape(N_SHARD, PROPOSAL_TOTAL)
        chosen_elements = keeper_positions[query_pass_number].reshape(N_SHARD, KEEPER_TOTAL)
        keep_mask = (chosen_elements < alive_tallies[query_pass_number][:, None]).astype(jnp.float32)
        sigmoid_factors = jax.nn.sigmoid(jnp.take_along_axis(scores, chosen_elements, axis=1)) * keep_mask
        modulated_vectors = (keeper_ordering_vectors[query_pass_number].reshape(N_SHARD, KEEPER_TOTAL, ORDERING_WIDTH).astype(jnp.float32) * sigmoid_factors[:, :, None]).astype(jnp.bfloat16)
        holder_labels = holder_shards[query_pass_number].reshape(N_SHARD, KEEPER_TOTAL)
        gain_rows = holder_attribute_factor[holder_labels.reshape(-1)].astype(jnp.float32)
        onehot = (holder_labels[:, :, None] == columns[None, None, :]).astype(jnp.int32)
        before = jnp.cumsum(onehot, axis=1) - onehot
        slot_within = jnp.sum(before * onehot, axis=2)
        sender_pos = holder_labels * SLOT_LIMIT + slot_within
        holder_position = sender_labels * SLOT_LIMIT + slot_within
        gate_slots = jnp.zeros((N_SHARD, PLACE_TOTAL), jnp.float32).at[sender_labels, sender_pos].set(sigmoid_factors)
        segment_lists[0].append(gate_slots.reshape(-1))
        present_matrix = modulated_vectors.reshape(N_SHARD * KEEPER_TOTAL, ORDERING_WIDTH)
        flag_vals = keep_mask.reshape(-1)
        for section_id in range(3):
            present_matrix, raw_activations = rank_section(present_matrix, flag_vals, gain_rows, block_lowering_matrices[section_id], block_raising_flipped[section_id], block_result_offsets[section_id], block_grading_vectors[section_id], section_id == 0)
            deposited_vectors = jnp.zeros((N_SHARD, PLACE_TOTAL), jnp.float32).at[holder_labels, holder_position].set(raw_activations.reshape(N_SHARD, KEEPER_TOTAL))
            segment_lists[section_id + 1].append(deposited_vectors.reshape(-1))
    return jnp.stack([jnp.stack(entry_list) for entry_list in segment_lists])
```

```python
import jax
import jax.numpy as jnp
from jax import lax
from jax.sharding import PartitionSpec as P

F32 = jnp.float32
BF16 = jnp.bfloat16
HIGH = lax.Precision.HIGHEST
LANES = 128


def fdot(a, b, precision=None):
    return jnp.dot(a, b, preferred_element_type=F32, precision=precision)


def gather_blocks(block):
    return lax.all_gather(block, "shard", axis=0, tiled=False)


def sum_segments(value):
    return lax.psum(value, "segment")


def local(
    proposal_attributes,
    keeper_ordering_vectors,
    keeper_positions,
    alive_tallies,
    holder_shards,
    holder_attribute_factor,
    early_inner_matrix,
    early_inner_offset,
    early_grading_vector,
    block_lowering_matrices,
    block_raising_flipped,
    block_result_offsets,
    block_grading_vectors,
):
    segment_id = lax.axis_index("segment")
    segment_count = lax.axis_size("segment")
    shard_count = lax.axis_size("shard")
    rounds, entries, width = keeper_ordering_vectors.shape
    candidates = proposal_attributes.shape[1]
    low_rank = block_lowering_matrices.shape[2]
    cap_slots = max(2, 2 * entries // shard_count)
    rows = rounds * entries
    own_features = width // shard_count
    piece = own_features // segment_count
    part_width = width // segment_count
    span = segment_count * LANES
    spans = width // span

    at = lax.broadcasted_iota(jnp.int32, (span, LANES), 0)
    to = lax.broadcasted_iota(jnp.int32, (span, LANES), 1)
    chosen = (at // own_features == to // piece) & (
        at % own_features == segment_id * piece + to % piece
    )
    pick = chosen.astype(BF16)
    pick32 = chosen.astype(F32)

    def part_of(values):
        return [fdot(values[:, g * span : (g + 1) * span], pick) for g in range(spans)]

    def part_of32(values):
        return jnp.concatenate(
            [fdot(values[:, g * span : (g + 1) * span], pick32, HIGH) for g in range(spans)], 1
        )

    own_gain = jnp.concatenate(part_of(holder_attribute_factor), 0).astype(BF16)
    own_lower = lax.dynamic_slice_in_dim(block_lowering_matrices, segment_id * piece, piece, 1)
    own_raise = lax.dynamic_slice_in_dim(block_raising_flipped, segment_id * piece, piece, 1)
    block = jnp.concatenate(
        [own_lower.reshape(3 * piece, low_rank), own_raise.reshape(3 * piece, low_rank), own_gain], 0
    )
    blocks = gather_blocks(block)

    def matrix(k):
        return blocks[:, k * piece : (k + 1) * piece].reshape(part_width, low_rank)

    hidden = jax.nn.relu(
        fdot(proposal_attributes.reshape(rounds * candidates, -1), early_inner_matrix)
        + early_inner_offset
    ).astype(BF16)
    scores = fdot(hidden, early_grading_vector).reshape(rounds, candidates)
    ids = jnp.arange(candidates, dtype=jnp.int32)
    looked_up = jnp.sum(
        jnp.where(keeper_positions[:, :, None] == ids, scores[:, None, :], 0.0), axis=2
    )
    keep = (keeper_positions < alive_tallies).astype(F32)
    gate = jax.nn.sigmoid(looked_up) * keep

    owner = holder_shards[:, :, 0]
    order = jnp.arange(entries, dtype=jnp.int32)
    same = (owner[:, :, None] == owner[:, None, :]) & (order[None, :] < order[:, None])
    within = jnp.sum(same.astype(jnp.int32), axis=2)
    target = owner * cap_slots + within
    slots = jnp.arange(shard_count * cap_slots, dtype=jnp.int32)
    placed = slots[None, :, None] == target[:, None, :]

    gate_col = gate.reshape(rows, 1)
    keep_col = keep.reshape(rows, 1)
    own_rows = jnp.concatenate(part_of(keeper_ordering_vectors.reshape(rows, width)), 1)
    h0 = (own_rows * gate_col).astype(BF16)
    owner_hot = (
        owner.reshape(rows, 1) == jnp.arange(shard_count, dtype=jnp.int32)[None, :]
    ).astype(BF16)
    gains = jnp.concatenate(
        [fdot(owner_hot, blocks[:, 6 * piece + g]) for g in range(part_width // LANES)], 1
    )
    x = (h0.astype(F32) * gains).astype(BF16)

    biases = part_of32(block_result_offsets)
    heads = part_of32(block_grading_vectors)
    lower1, lower2, lower3, raise1, raise2, raise3 = [matrix(k) for k in range(6)]

    between = lax.dot_general(
        raise2, lower3, (((0,), (0,)), ((), ())), preferred_element_type=F32
    )
    raised = lax.dot_general(
        heads[1:3], raise2.astype(F32), (((1,), (0,)), ((), ())), precision=HIGH
    )
    raised3 = lax.dot_general(
        heads[2:3], raise3.astype(F32), (((1,), (0,)), ((), ())), precision=HIGH
    )
    lowered_bias = lax.dot_general(
        biases[1:2], lower3.astype(F32), (((1,), (0,)), ((), ())), precision=HIGH
    )
    consts = jnp.stack(
        [
            jnp.sum(biases[1] * heads[1]),
            jnp.sum(biases[1] * heads[2]),
            jnp.sum(biases[2] * heads[2]),
        ]
    )
    consts = jnp.pad(consts, (0, low_rank - 3))[None]
    first = jnp.concatenate(
        [fdot(x, lower1), between, raised, raised3, lowered_bias, consts], 0
    )
    first = sum_segments(jnp.pad(first, ((0, 3), (0, 0))))

    act1 = first[:rows].astype(BF16)
    lifted = (
        lax.dot_general(act1, raise1, (((1,), (1,)), ((), ())), preferred_element_type=F32)
        + biases[0]
    )
    x32 = x.astype(F32)
    out1 = (x32 + x32 * lifted) * keep_col
    h1 = out1.astype(BF16)
    h1_32 = h1.astype(F32)
    graded = jnp.stack(
        [
            jnp.sum(out1 * heads[0], axis=1),
            jnp.sum(h1_32 * heads[1], axis=1),
            jnp.sum(h1_32 * heads[2], axis=1),
        ]
    ).reshape(-1, low_rank)
    second = jnp.concatenate([fdot(h1, lower2), fdot(h1, lower3), graded], 0)
    second = sum_segments(jnp.pad(second, ((0, -second.shape[0] % 8), (0, 0))))

    between = first[rows : rows + low_rank]
    vectors = first[rows + low_rank : rows + low_rank + 5]
    graded = second[2 * rows : 2 * rows + 3 * rows // low_rank].reshape(3, rows)
    keep_row = keep.reshape(rows)
    act2 = jax.nn.relu(second[:rows]).astype(BF16).astype(F32)
    graded2 = graded[1] + jnp.sum(act2 * vectors[0], axis=1) + vectors[4, 0]
    inner3 = (second[rows : 2 * rows] + fdot(act2, between, HIGH) + vectors[3]) * keep_col
    act3 = jax.nn.relu(inner3).astype(BF16).astype(F32)
    graded3 = (
        (graded[2] + jnp.sum(act2 * vectors[1], axis=1) + vectors[4, 1]) * keep_row
        + jnp.sum(act3 * vectors[2], axis=1)
        + vectors[4, 2]
    )
    section = jnp.stack([gate.reshape(rows), graded[0], graded2 * keep_row, graded3 * keep_row])
    values = lax.dynamic_index_in_dim(section, segment_id, 0, keepdims=False)
    values = values.reshape(rounds, 1, entries)
    sent = jnp.sum(jnp.where(placed, values, 0.0), axis=2)
    outgoing = sent.reshape(rounds, shard_count, cap_slots).transpose(1, 0, 2)
    outgoing = outgoing.reshape(shard_count, rounds * cap_slots)
    arrived = lax.all_to_all(outgoing, "shard", split_axis=0, concat_axis=0, tiled=True)
    arrived = arrived.reshape(shard_count, rounds, cap_slots).transpose(1, 0, 2)
    arrived = arrived.reshape(rounds, shard_count * cap_slots)
    return jnp.where(segment_id == 0, sent, arrived)[None]


def solution(mesh):
    placed = (
        P(None, "shard", None),
        P(None, "shard", None),
        P(None, "shard"),
        P(None, "shard"),
        P(None, "shard", None),
        P("shard", None),
        P(),
        P(),
        P(),
        P(None, "shard", None),
        P(None, "shard", None),
        P(),
        P(),
    )
    return jax.shard_map(
        local, mesh=mesh, in_specs=placed, out_specs=P("segment", None, "shard"), check_vma=False
    )
```

```python
import functools
import math

import jax
import jax.numpy as jnp
from jax import lax
from jax.experimental import pallas as pl
from jax.experimental.pallas import tpu as pltpu
from jax.sharding import PartitionSpec as P

F32 = jnp.float32
BF16 = jnp.bfloat16
HIGH = lax.Precision.HIGHEST
LANES = 128


def fdot(a, b, precision=None):
    return jnp.dot(a, b, preferred_element_type=F32, precision=precision)


MESH = pl.DeviceIdType.MESH


def gather_kernel(side, count, *refs):
    ins, outs = refs[:count], refs[count : 2 * count]
    own_sem, near_send, near_recv, far_send, far_recv, core_send, core_recv = refs[2 * count :]
    segment = lax.axis_index("segment")
    me = lax.axis_index("shard")
    core = lax.rem(me, 2)
    y = lax.rem(me // 2, side)
    z = me // (2 * side)

    def device(zz, yy, cc):
        return (segment, (zz * side + yy) * 2 + cc)

    def turned(value, by):
        return lax.rem(value + by + side, side)

    y_peers = [None] + [device(z, turned(y, k), core) for k in range(1, side)]
    z_peers = [None] + [device(turned(z, k), y, core) for k in range(1, side)]
    partner = device(z, y, 1 - core)

    barrier = pltpu.get_barrier_semaphore()
    for peer in y_peers[1:] + z_peers[1:] + [partner]:
        pl.semaphore_signal(barrier, inc=1, device_id=peer, device_id_type=MESH)
    pl.semaphore_wait(barrier, 2 * side - 1)

    def slab(i, k):
        if i == 0:
            return outs[i].at[turned(z, -k), :, core]
        return outs[i].at[:, turned(y, -k), core]

    def send(src, dst, send_sem, recv_sem, peer):
        copy = pltpu.make_async_remote_copy(
            src_ref=src,
            dst_ref=dst,
            send_sem=send_sem,
            recv_sem=recv_sem,
            device_id=peer,
            device_id_type=MESH,
        )
        copy.start()
        return copy

    near, far, across, own = {}, {}, {}, {}
    for k in range(1, side):
        for i in range(count):
            peers = y_peers if i == 0 else z_peers
            near[i, k] = send(
                ins[i], outs[i].at[z, y, core], near_send.at[i, k], near_recv.at[i, k], peers[k]
            )
    for i in range(count):
        own[i] = pltpu.make_async_copy(ins[i], outs[i].at[z, y, core], own_sem.at[i])
        own[i].start()
    for i in range(count):
        own[i].wait()
        for k in range(1, side):
            near[i, k].wait()
        peers = z_peers if i == 0 else y_peers
        for k in range(1, side):
            far[i, k] = send(
                slab(i, 0), slab(i, 0), far_send.at[i, k], far_recv.at[i, k], peers[k]
            )
        across[i, 0] = send(
            slab(i, 0), slab(i, 0), core_send.at[i, 0], core_recv.at[i, 0], partner
        )
    for k in range(1, side):
        for i in range(count):
            far[i, k].wait()
            across[i, k] = send(
                slab(i, k), slab(i, k), core_send.at[i, k], core_recv.at[i, k], partner
            )
    for k in range(side):
        for i in range(count):
            across[i, k].wait()


def gather_blocks(first, second, collective_id):
    shard_count = lax.axis_size("shard")
    side = math.isqrt(shard_count // 2)
    sems = pltpu.SemaphoreType.DMA((2, side))
    outs = pl.pallas_call(
        functools.partial(gather_kernel, side, 2),
        out_shape=[
            jax.ShapeDtypeStruct((side, side, 2) + b.shape, b.dtype) for b in (first, second)
        ],
        in_specs=[pl.BlockSpec(memory_space=pltpu.VMEM)] * 2,
        out_specs=[pl.BlockSpec(memory_space=pltpu.VMEM)] * 2,
        scratch_shapes=[pltpu.SemaphoreType.DMA((2,))] + [sems] * 6,
        compiler_params=pltpu.CompilerParams(collective_id=collective_id, has_side_effects=True),
    )(first, second)
    return [o.reshape((shard_count,) + o.shape[3:]) for o in outs]


def sum_kernel(count, x_ref, out_ref, slots, own_sem, send_sem, recv_sem):
    segment = lax.axis_index("segment")
    me = lax.axis_index("shard")
    peers = [(lax.rem(segment + k, count), me) for k in range(1, count)]
    barrier = pltpu.get_barrier_semaphore()
    for peer in peers:
        pl.semaphore_signal(barrier, inc=1, device_id=peer, device_id_type=MESH)
    pl.semaphore_wait(barrier, count - 1)
    copies = []
    for k, peer in enumerate(peers):
        copies.append(
            pltpu.make_async_remote_copy(
                src_ref=x_ref,
                dst_ref=slots.at[segment],
                send_sem=send_sem.at[k],
                recv_sem=recv_sem.at[k],
                device_id=peer,
                device_id_type=MESH,
            )
        )
        copies[-1].start()
    own = pltpu.make_async_copy(x_ref, slots.at[segment], own_sem)
    own.start()
    own.wait()
    for copy in copies:
        copy.wait()
    total = slots[0]
    for k in range(1, count):
        total = total + slots[k]
    out_ref[...] = total


def sum_segments(value, collective_id):
    count = lax.axis_size("segment")
    return pl.pallas_call(
        functools.partial(sum_kernel, count),
        out_shape=jax.ShapeDtypeStruct(value.shape, value.dtype),
        in_specs=[pl.BlockSpec(memory_space=pltpu.VMEM)],
        out_specs=pl.BlockSpec(memory_space=pltpu.VMEM),
        scratch_shapes=[
            pltpu.VMEM((count,) + value.shape, value.dtype),
            pltpu.SemaphoreType.DMA,
            pltpu.SemaphoreType.DMA((count - 1,)),
            pltpu.SemaphoreType.DMA((count - 1,)),
        ],
        compiler_params=pltpu.CompilerParams(collective_id=collective_id, has_side_effects=True),
    )(value)


def local(
    proposal_attributes,
    keeper_ordering_vectors,
    keeper_positions,
    alive_tallies,
    holder_shards,
    holder_attribute_factor,
    early_inner_matrix,
    early_inner_offset,
    early_grading_vector,
    block_lowering_matrices,
    block_raising_flipped,
    block_result_offsets,
    block_grading_vectors,
):
    segment_id = lax.axis_index("segment")
    segment_count = lax.axis_size("segment")
    shard_count = lax.axis_size("shard")
    rounds, entries, width = keeper_ordering_vectors.shape
    candidates = proposal_attributes.shape[1]
    low_rank = block_lowering_matrices.shape[2]
    cap_slots = max(2, 2 * entries // shard_count)
    rows = rounds * entries
    own_features = width // shard_count
    piece = own_features // segment_count
    part_width = width // segment_count
    span = segment_count * LANES
    spans = width // span

    at = lax.broadcasted_iota(jnp.int32, (span, LANES), 0)
    to = lax.broadcasted_iota(jnp.int32, (span, LANES), 1)
    chosen = (at // own_features == to // piece) & (
        at % own_features == segment_id * piece + to % piece
    )
    pick = chosen.astype(BF16)
    pick32 = chosen.astype(F32)

    def part_of(values):
        return [fdot(values[:, g * span : (g + 1) * span], pick) for g in range(spans)]

    wide = jnp.concatenate(
        [holder_attribute_factor.astype(F32), block_result_offsets, block_grading_vectors], 0
    )
    wide = fdot(wide.reshape(7 * spans, span), pick32, HIGH)
    own_gain = wide[:spans].astype(BF16)
    wide = wide[spans:].reshape(6, part_width)
    biases, heads = wide[:3], wide[3:]
    own_lower = lax.dynamic_slice_in_dim(block_lowering_matrices, segment_id * piece, piece, 1)
    own_raise = lax.dynamic_slice_in_dim(block_raising_flipped, segment_id * piece, piece, 1)
    lower_blocks, raise_blocks = gather_blocks(
        own_lower.reshape(3 * piece, low_rank),
        jnp.concatenate([own_raise.reshape(3 * piece, low_rank), own_gain], 0),
        0,
    )

    def matrix(blocks, k):
        return blocks[:, k * piece : (k + 1) * piece].reshape(part_width, low_rank)

    hidden = jax.nn.relu(
        fdot(proposal_attributes.reshape(rounds * candidates, -1), early_inner_matrix)
        + early_inner_offset
    ).astype(BF16)
    scores = fdot(hidden, early_grading_vector).reshape(rounds, candidates)
    ids = jnp.arange(candidates, dtype=jnp.int32)
    looked_up = jnp.sum(
        jnp.where(keeper_positions[:, :, None] == ids, scores[:, None, :], 0.0), axis=2
    )
    keep = (keeper_positions < alive_tallies).astype(F32)
    gate = jax.nn.sigmoid(looked_up) * keep

    owner = holder_shards[:, :, 0]
    order = jnp.arange(entries, dtype=jnp.int32)
    same = (owner[:, :, None] == owner[:, None, :]) & (order[None, :] < order[:, None])
    within = jnp.sum(same.astype(jnp.int32), axis=2)
    owners = jnp.arange(shard_count, dtype=jnp.int32)
    places = jnp.arange(cap_slots, dtype=jnp.int32)
    placed = (owner[:, None, None, :] == owners[:, None]) & (
        within[:, None, None, :] == places[:, None, None]
    )

    gate_col = gate.reshape(rows, 1)
    keep_col = keep.reshape(rows, 1)
    own_rows = jnp.concatenate(part_of(keeper_ordering_vectors.reshape(rows, width)), 1)
    h0 = (own_rows * gate_col).astype(BF16)
    owner_hot = (
        owner.reshape(rows, 1) == jnp.arange(shard_count, dtype=jnp.int32)[None, :]
    ).astype(BF16)
    gains = jnp.concatenate(
        [fdot(owner_hot, raise_blocks[:, 3 * piece + g]) for g in range(part_width // LANES)], 1
    )
    x = (h0.astype(F32) * gains).astype(BF16)

    lower1, lower2, lower3 = [matrix(lower_blocks, k) for k in range(3)]
    raise1, raise2, raise3 = [matrix(raise_blocks, k) for k in range(3)]

    between = lax.dot_general(
        raise2, lower3, (((0,), (0,)), ((), ())), preferred_element_type=F32
    )
    raised = lax.dot_general(
        heads[1:3], raise2.astype(F32), (((1,), (0,)), ((), ())), precision=HIGH
    )
    raised3 = lax.dot_general(
        heads[2:3], raise3.astype(F32), (((1,), (0,)), ((), ())), precision=HIGH
    )
    lowered_bias = lax.dot_general(
        biases[1:2], lower3.astype(F32), (((1,), (0,)), ((), ())), precision=HIGH
    )
    consts = jnp.stack(
        [
            jnp.sum(biases[1] * heads[1]),
            jnp.sum(biases[1] * heads[2]),
            jnp.sum(biases[2] * heads[2]),
        ]
    )
    consts = jnp.pad(consts, (0, low_rank - 3))[None]
    first = jnp.concatenate(
        [fdot(x, lower1), between, raised, raised3, lowered_bias, consts], 0
    )
    first = sum_segments(jnp.pad(first, ((0, 3), (0, 0))), 1)

    act1 = first[:rows].astype(BF16)
    lifted = (
        lax.dot_general(act1, raise1, (((1,), (1,)), ((), ())), preferred_element_type=F32)
        + biases[0]
    )
    x32 = x.astype(F32)
    out1 = (x32 + x32 * lifted) * keep_col
    h1 = out1.astype(BF16)
    h1_32 = h1.astype(F32)
    graded = jnp.stack(
        [
            jnp.sum(out1 * heads[0], axis=1),
            jnp.sum(h1_32 * heads[1], axis=1),
            jnp.sum(h1_32 * heads[2], axis=1),
        ]
    ).reshape(-1, low_rank)
    second = jnp.concatenate([fdot(h1, lower2), fdot(h1, lower3), graded], 0)
    second = sum_segments(jnp.pad(second, ((0, -second.shape[0] % 8), (0, 0))), 2)

    between = first[rows : rows + low_rank]
    vectors = first[rows + low_rank : rows + low_rank + 5]
    graded = second[2 * rows : 2 * rows + 3 * rows // low_rank].reshape(3, rows)
    keep_row = keep.reshape(rows)
    act2 = jax.nn.relu(second[:rows]).astype(BF16).astype(F32)
    graded2 = graded[1] + jnp.sum(act2 * vectors[0], axis=1) + vectors[4, 0]
    inner3 = (second[rows : 2 * rows] + fdot(act2, between, HIGH) + vectors[3]) * keep_col
    act3 = jax.nn.relu(inner3).astype(BF16).astype(F32)
    graded3 = (
        (graded[2] + jnp.sum(act2 * vectors[1], axis=1) + vectors[4, 1]) * keep_row
        + jnp.sum(act3 * vectors[2], axis=1)
        + vectors[4, 2]
    )
    section = jnp.stack([gate.reshape(rows), graded[0], graded2 * keep_row, graded3 * keep_row])
    values = lax.dynamic_index_in_dim(section, segment_id, 0, keepdims=False)
    values = values.reshape(rounds, 1, 1, entries)
    sent = jnp.sum(jnp.where(placed, values, 0.0), axis=3)
    boards = jnp.stack(gather_blocks(sent[0], sent[1], 3))
    mine = owners == lax.axis_index("shard")
    arrived = jnp.sum(jnp.where(mine, boards, 0.0), axis=3)
    result = jnp.where(segment_id == 0, sent.transpose(0, 2, 1), arrived)
    return result.reshape(1, rounds, shard_count * cap_slots)


def solution(mesh):
    placed = (
        P(None, "shard", None),
        P(None, "shard", None),
        P(None, "shard"),
        P(None, "shard"),
        P(None, "shard", None),
        P("shard", None),
        P(),
        P(),
        P(),
        P(None, "shard", None),
        P(None, "shard", None),
        P(),
        P(),
    )
    return jax.shard_map(
        local, mesh=mesh, in_specs=placed, out_specs=P("segment", None, "shard"), check_vma=False
    )
```

```python
import functools
import math

import jax
import jax.numpy as jnp
from jax import lax
from jax.experimental import pallas as pl
from jax.experimental.pallas import tpu as pltpu
from jax.sharding import PartitionSpec as P

F32 = jnp.float32
BF16 = jnp.bfloat16
HIGH = lax.Precision.HIGHEST
LANES = 128


def fdot(a, b, precision=None):
    return jnp.dot(a, b, preferred_element_type=F32, precision=precision)


MESH = pl.DeviceIdType.MESH


def gather_kernel(side, count, extra_in, extra_out, works, *refs):
    ins, given = refs[:count], refs[count : count + extra_in]
    refs = refs[count + extra_in :]
    outs, made = refs[:count], refs[count : count + extra_out]
    refs = refs[count + extra_out :]
    own_sem, near_send, near_recv, far_send, far_recv, core_send, core_recv = refs[:7]
    scratch = refs[7:]
    segment = lax.axis_index("segment")
    me = lax.axis_index("shard")
    core = lax.rem(me, 2)
    y = lax.rem(me // 2, side)
    z = me // (2 * side)

    def device(zz, yy, cc):
        return (segment, (zz * side + yy) * 2 + cc)

    def turned(value, by):
        return lax.rem(value + by + side, side)

    y_peers = [None] + [device(z, turned(y, k), core) for k in range(1, side)]
    z_peers = [None] + [device(turned(z, k), y, core) for k in range(1, side)]
    partner = device(z, y, 1 - core)

    barrier = pltpu.get_barrier_semaphore()
    for peer in y_peers[1:] + z_peers[1:] + [partner]:
        pl.semaphore_signal(barrier, inc=1, device_id=peer, device_id_type=MESH)
    pl.semaphore_wait(barrier, 2 * side - 1)

    def slab(i, k):
        if i == 0:
            return outs[i].at[turned(z, -k), :, core]
        return outs[i].at[:, turned(y, -k), core]

    def send(src, dst, send_sem, recv_sem, peer):
        copy = pltpu.make_async_remote_copy(
            src_ref=src,
            dst_ref=dst,
            send_sem=send_sem,
            recv_sem=recv_sem,
            device_id=peer,
            device_id_type=MESH,
        )
        copy.start()
        return copy

    near, far, across, own = {}, {}, {}, {}
    for k in range(1, side):
        for i in range(count):
            peers = y_peers if i == 0 else z_peers
            near[i, k] = send(
                ins[i], outs[i].at[z, y, core], near_send.at[i, k], near_recv.at[i, k], peers[k]
            )
    for i in range(count):
        own[i] = pltpu.make_async_copy(ins[i], outs[i].at[z, y, core], own_sem.at[i])
        own[i].start()
    if works:
        works[0](given, made, scratch)
    for i in range(count):
        own[i].wait()
        for k in range(1, side):
            near[i, k].wait()
        peers = z_peers if i == 0 else y_peers
        for k in range(1, side):
            far[i, k] = send(
                slab(i, 0), slab(i, 0), far_send.at[i, k], far_recv.at[i, k], peers[k]
            )
        across[i, 0] = send(
            slab(i, 0), slab(i, 0), core_send.at[i, 0], core_recv.at[i, 0], partner
        )
    if works:
        works[1](given, made, scratch)
    for k in range(1, side):
        for i in range(count):
            far[i, k].wait()
            across[i, k] = send(
                slab(i, k), slab(i, k), core_send.at[i, k], core_recv.at[i, k], partner
            )
    for k in range(side):
        for i in range(count):
            across[i, k].wait()


def gather_blocks(first, second, collective_id, given=(), made=(), scratch=(), works=None):
    shard_count = lax.axis_size("shard")
    side = math.isqrt(shard_count // 2)
    sems = pltpu.SemaphoreType.DMA((2, side))
    outs = pl.pallas_call(
        functools.partial(gather_kernel, side, 2, len(given), len(made), works),
        out_shape=[
            jax.ShapeDtypeStruct((side, side, 2) + b.shape, b.dtype) for b in (first, second)
        ]
        + list(made),
        in_specs=[pl.BlockSpec(memory_space=pltpu.VMEM)] * (2 + len(given)),
        out_specs=[pl.BlockSpec(memory_space=pltpu.VMEM)] * (2 + len(made)),
        scratch_shapes=[pltpu.SemaphoreType.DMA((2,))] + [sems] * 6 + list(scratch),
        compiler_params=pltpu.CompilerParams(
            collective_id=collective_id, has_side_effects=True, vmem_limit_bytes=48 * 2**20
        ),
    )(first, second, *given)
    return [o.reshape((shard_count,) + o.shape[3:]) for o in outs[:2]] + list(outs[2:])


def prerank_work(given, made, scratch):
    attributes, inner, offset, grading = given[:4]
    (scores,) = scratch

    def step(t, carry):
        block = attributes[pl.ds(pl.multiple_of(t * LANES, LANES), LANES), :]
        hidden = jnp.maximum(fdot(block, inner[...]) + offset[...], 0.0).astype(BF16)
        scores[t] = lax.dot_general(
            grading[...], hidden, (((1,), (1,)), ((), ())), preferred_element_type=F32
        )
        return carry

    lax.fori_loop(0, attributes.shape[0] // LANES, step, 0)


def gate_work(rounds, given, made, scratch):
    positions, keep, rows, pick = given[4:]
    gates, gated = made
    (scores,) = scratch
    entries = rows.shape[0] // rounds
    steps = scores.shape[0] // rounds
    span = pick.shape[0]
    for r in range(rounds):
        here = pl.ds(r * entries, entries)
        looked_up = jnp.zeros((entries, LANES), F32)
        for t in range(steps):
            ids = lax.broadcasted_iota(jnp.int32, (entries, LANES), 1) + t * LANES
            row = scores[r * steps + t][0:1, :]
            looked_up += jnp.where(positions[here, :] == ids, row, 0.0)
        score = jnp.sum(looked_up, axis=1, keepdims=True)
        small = jnp.exp(-jnp.abs(score))
        gate = keep[here, :] * jnp.where(score >= 0.0, 1.0, small) / (1.0 + small)
        gates[here, :] = gate
        for g in range(rows.shape[1] // span):
            part = fdot(rows[here, g * span : (g + 1) * span], pick[...])
            gated[here, g * LANES : (g + 1) * LANES] = (part * gate).astype(BF16)


NT = (((1,), (1,)), ((), ()))


def section_kernel(
    count,
    h0,
    keep,
    keep_row,
    owner,
    gain,
    wide,
    lower1,
    lower2,
    lower3,
    raise1,
    raise2,
    raise3,
    out_ref,
    x_ref,
    out1_ref,
    slots1,
    slots2,
    slots3,
    send_sem,
    recv_sem,
):
    segment = lax.axis_index("segment")
    me = lax.axis_index("shard")
    rows, width = x_ref.shape
    low_rank = lower1.shape[1]
    owners = gain.shape[0] * LANES // width
    per = width // LANES
    peers = [(lax.rem(segment + k, count), me) for k in range(1, count)]
    barrier = pltpu.get_barrier_semaphore()
    for peer in peers:
        pl.semaphore_signal(barrier, inc=1, device_id=peer, device_id_type=MESH)

    def exchange(number, slots):
        copies = []
        for k, peer in enumerate(peers):
            copies.append(
                pltpu.make_async_remote_copy(
                    src_ref=slots.at[segment],
                    dst_ref=slots.at[segment],
                    send_sem=send_sem.at[number, k],
                    recv_sem=recv_sem.at[number, k],
                    device_id=peer,
                    device_id_type=MESH,
                )
            )
            copies[-1].start()
        return copies

    def total(slots, start, size):
        value = slots[0, start : start + size]
        for k in range(1, count):
            value = value + slots[k, start : start + size]
        return value

    owner_hot = (
        owner[...] == lax.broadcasted_iota(jnp.int32, (rows, owners), 1)
    ).astype(F32).astype(BF16)
    for g in range(per):
        gain_g = gain[pl.ds(g, owners, stride=per), :].astype(BF16)
        lanes = slice(g * LANES, (g + 1) * LANES)
        x_ref[:, lanes] = (h0[:, lanes].astype(F32) * fdot(owner_hot, gain_g)).astype(BF16)
    slots1[segment] = fdot(x_ref[...], lower1[...])
    pl.semaphore_wait(barrier, count - 1)
    first = exchange(0, slots1)

    table = wide[...]
    slots2[segment, 0:low_rank] = lax.dot_general(
        raise2[...], lower3[...], (((0,), (0,)), ((), ())), preferred_element_type=F32
    )
    for n, matrix in enumerate((raise2, raise3, lower3)):
        at = low_rank + 8 * n
        slots2[segment, at : at + 8] = fdot(table, matrix[...].astype(F32), HIGH)
    consts = [
        jnp.sum(table[a : a + 1] * table[b : b + 1], axis=1, keepdims=True)
        for a, b in ((1, 4), (1, 5), (2, 5))
    ]
    row = lax.broadcasted_iota(jnp.int32, (8, low_rank), 0)
    slots2[segment, low_rank + 24 : low_rank + 32] = jnp.where(
        row == 0, consts[0], jnp.where(row == 1, consts[1], consts[2])
    )
    for copy in first:
        copy.wait()
    weights = exchange(1, slots2)

    act1 = total(slots1, 0, rows).astype(BF16)
    for g in range(per):
        lanes = slice(g * LANES, (g + 1) * LANES)
        lifted = (
            lax.dot_general(act1, raise1[lanes, :], NT, preferred_element_type=F32)
            + table[0:1, lanes]
        )
        x32 = x_ref[:, lanes].astype(F32)
        out1 = (x32 + x32 * lifted) * keep[...]
        out1_ref[:, lanes] = out1
        x_ref[:, lanes] = out1.astype(BF16)
    h1 = x_ref[...]
    slots3[segment, 0:rows] = fdot(h1, lower2[...])
    slots3[segment, rows : 2 * rows] = fdot(h1, lower3[...])
    graded1 = lax.dot_general(table, out1_ref[...], NT, precision=HIGH, preferred_element_type=F32)
    graded = lax.dot_general(
        table, h1.astype(F32), NT, precision=HIGH, preferred_element_type=F32
    )
    which = lax.broadcasted_iota(jnp.int32, graded.shape, 0)
    graded = jnp.where(which == 3, graded1, graded)
    for c in range(rows // LANES):
        at = 2 * rows + 8 * c
        slots3[segment, at : at + 8] = graded[:, c * LANES : (c + 1) * LANES]
    for copy in weights:
        copy.wait()
    between = total(slots2, 0, low_rank)
    raised2 = total(slots2, low_rank, 8)
    raised3 = total(slots2, low_rank + 8, 8)
    lowered = total(slots2, low_rank + 16, 8)
    consts = total(slots2, low_rank + 24, 8)
    for copy in exchange(2, slots3):
        copy.wait()

    act2 = jnp.maximum(total(slots3, 0, rows), 0.0).astype(BF16).astype(F32)
    inner3 = (
        total(slots3, rows, rows) + fdot(act2, between, HIGH) + lowered[1:2]
    ) * keep[...]
    act3 = jnp.maximum(inner3, 0.0).astype(BF16).astype(F32)
    from2 = lax.dot_general(raised2, act2, NT, precision=HIGH, preferred_element_type=F32)
    from3 = lax.dot_general(raised3, act3, NT, precision=HIGH, preferred_element_type=F32)
    for c in range(rows // LANES):
        lanes = slice(c * LANES, (c + 1) * LANES)
        graded = total(slots3, 2 * rows + 8 * c, 8)
        kept = keep_row[0:1, lanes]
        out_ref[0:1, lanes] = graded[3:4]
        out_ref[1:2, lanes] = (graded[4:5] + from2[4:5, lanes] + consts[0:1]) * kept
        out_ref[2:3, lanes] = (
            (graded[5:6] + from2[5:6, lanes] + consts[1:2]) * kept
            + from3[5:6, lanes]
            + consts[2:3]
        ) * kept


def run_sections(collective_id, *operands):
    count = lax.axis_size("segment")
    rows, width = operands[0].shape
    low_rank = operands[6].shape[1]
    sems = pltpu.SemaphoreType.DMA((3, count - 1))
    return pl.pallas_call(
        functools.partial(section_kernel, count),
        out_shape=jax.ShapeDtypeStruct((3, rows), F32),
        in_specs=[pl.BlockSpec(memory_space=pltpu.VMEM)] * len(operands),
        out_specs=pl.BlockSpec(memory_space=pltpu.VMEM),
        scratch_shapes=[
            pltpu.VMEM((rows, width), BF16),
            pltpu.VMEM((rows, width), F32),
            pltpu.VMEM((count, rows, low_rank), F32),
            pltpu.VMEM((count, low_rank + 32, low_rank), F32),
            pltpu.VMEM((count, 2 * rows + rows // LANES * 8, low_rank), F32),
            sems,
            sems,
        ],
        compiler_params=pltpu.CompilerParams(
            collective_id=collective_id, has_side_effects=True, vmem_limit_bytes=48 * 2**20
        ),
    )(*operands)


def local(
    proposal_attributes,
    keeper_ordering_vectors,
    keeper_positions,
    alive_tallies,
    holder_shards,
    holder_attribute_factor,
    early_inner_matrix,
    early_inner_offset,
    early_grading_vector,
    block_lowering_matrices,
    block_raising_flipped,
    block_result_offsets,
    block_grading_vectors,
):
    segment_id = lax.axis_index("segment")
    segment_count = lax.axis_size("segment")
    shard_count = lax.axis_size("shard")
    rounds, entries, width = keeper_ordering_vectors.shape
    candidates = proposal_attributes.shape[1]
    low_rank = block_lowering_matrices.shape[2]
    cap_slots = max(2, 2 * entries // shard_count)
    rows = rounds * entries
    own_features = width // shard_count
    piece = own_features // segment_count
    part_width = width // segment_count
    span = segment_count * LANES
    spans = width // span

    at = lax.broadcasted_iota(jnp.int32, (span, LANES), 0)
    to = lax.broadcasted_iota(jnp.int32, (span, LANES), 1)
    chosen = (at // own_features == to // piece) & (
        at % own_features == segment_id * piece + to % piece
    )
    pick = chosen.astype(BF16)
    pick32 = chosen.astype(F32)

    wide = jnp.concatenate(
        [holder_attribute_factor.astype(F32), block_result_offsets, block_grading_vectors], 0
    )
    wide = fdot(wide.reshape(7 * spans, span), pick32, HIGH)
    own_gain = wide[:spans].astype(BF16)
    wide = wide[spans:].reshape(6, part_width)
    own_lower = lax.dynamic_slice_in_dim(block_lowering_matrices, segment_id * piece, piece, 1)
    own_raise = lax.dynamic_slice_in_dim(block_raising_flipped, segment_id * piece, piece, 1)
    owner = holder_shards[:, :, 0]
    keep = (keeper_positions < alive_tallies).astype(F32)
    keep_col = keep.reshape(rows, 1)
    lower_blocks, raise_blocks, gate_col, h0 = gather_blocks(
        own_lower.reshape(3 * piece, low_rank),
        jnp.concatenate([own_raise.reshape(3 * piece, low_rank), own_gain], 0),
        0,
        (
            proposal_attributes.reshape(rounds * candidates, -1),
            early_inner_matrix,
            early_inner_offset[None],
            jnp.broadcast_to(early_grading_vector, (8,) + early_grading_vector.shape),
            keeper_positions.reshape(rows, 1),
            keep_col,
            keeper_ordering_vectors.reshape(rows, width),
            pick,
        ),
        (
            jax.ShapeDtypeStruct((rows, 1), F32),
            jax.ShapeDtypeStruct((rows, part_width), BF16),
        ),
        (pltpu.VMEM((rounds * candidates // LANES, 8, LANES), F32),),
        (prerank_work, functools.partial(gate_work, rounds)),
    )

    def matrix(blocks, k):
        return blocks[:, k * piece : (k + 1) * piece].reshape(part_width, low_rank)

    order = jnp.arange(entries, dtype=jnp.int32)
    same = (owner[:, :, None] == owner[:, None, :]) & (order[None, :] < order[:, None])
    within = jnp.sum(same.astype(jnp.int32), axis=2)
    owners = jnp.arange(shard_count, dtype=jnp.int32)
    places = jnp.arange(cap_slots, dtype=jnp.int32)
    placed = (owner[:, None, None, :] == owners[:, None]) & (
        within[:, None, None, :] == places[:, None, None]
    )

    gain = raise_blocks[:, 3 * piece :].astype(F32).reshape(-1, LANES)
    graded = run_sections(
        1,
        h0,
        keep_col,
        keep.reshape(1, rows),
        owner.reshape(rows, 1),
        gain,
        jnp.pad(wide, ((0, 2), (0, 0))),
        *[matrix(lower_blocks, k) for k in range(3)],
        *[matrix(raise_blocks, k) for k in range(3)],
    )
    section = jnp.concatenate([gate_col.reshape(1, rows), graded], 0)
    values = lax.dynamic_index_in_dim(section, segment_id, 0, keepdims=False)
    values = values.reshape(rounds, 1, 1, entries)
    sent = jnp.sum(jnp.where(placed, values, 0.0), axis=3)
    boards = jnp.stack(gather_blocks(sent[0], sent[1], 3))
    mine = owners == lax.axis_index("shard")
    arrived = jnp.sum(jnp.where(mine, boards, 0.0), axis=3)
    result = jnp.where(segment_id == 0, sent.transpose(0, 2, 1), arrived)
    return result.reshape(1, rounds, shard_count * cap_slots)


def solution(mesh):
    placed = (
        P(None, "shard", None),
        P(None, "shard", None),
        P(None, "shard"),
        P(None, "shard"),
        P(None, "shard", None),
        P("shard", None),
        P(),
        P(),
        P(),
        P(None, "shard", None),
        P(None, "shard", None),
        P(),
        P(),
    )
    return jax.shard_map(
        local, mesh=mesh, in_specs=placed, out_specs=P("segment", None, "shard"), check_vma=False
    )
```

```python
import functools
import math

import jax
import jax.numpy as jnp
from jax import lax
from jax.experimental import pallas as pl
from jax.experimental.pallas import tpu as pltpu
from jax.sharding import PartitionSpec as P

F32 = jnp.float32
BF16 = jnp.bfloat16
HIGH = lax.Precision.HIGHEST
LANES = 128


def fdot(a, b, precision=None):
    return jnp.dot(a, b, preferred_element_type=F32, precision=precision)


MESH = pl.DeviceIdType.MESH


def gather_kernel(side, count, extra_in, extra_out, works, *refs):
    ins, given = refs[:count], refs[count : count + extra_in]
    refs = refs[count + extra_in :]
    outs, made = refs[:count], refs[count : count + extra_out]
    refs = refs[count + extra_out :]
    own_sem, near_send, near_recv, far_send, far_recv, core_send, core_recv = refs[:7]
    scratch = refs[7:]
    segment = lax.axis_index("segment")
    me = lax.axis_index("shard")
    core = lax.rem(me, 2)
    y = lax.rem(me // 2, side)
    z = me // (2 * side)

    def device(zz, yy, cc):
        return (segment, (zz * side + yy) * 2 + cc)

    def turned(value, by):
        return lax.rem(value + by + side, side)

    y_peers = [None] + [device(z, turned(y, k), core) for k in range(1, side)]
    z_peers = [None] + [device(turned(z, k), y, core) for k in range(1, side)]
    partner = device(z, y, 1 - core)

    barrier = pltpu.get_barrier_semaphore()
    for peer in y_peers[1:] + z_peers[1:] + [partner]:
        pl.semaphore_signal(barrier, inc=1, device_id=peer, device_id_type=MESH)
    pl.semaphore_wait(barrier, 2 * side - 1)

    def slab(i, k, start=0, size=side):
        if i == 0:
            return outs[i].at[turned(z, -k), pl.ds(start, size), core]
        return outs[i].at[pl.ds(start, size), turned(y, -k), core]

    def send(src, dst, send_sem, recv_sem, peer):
        copy = pltpu.make_async_remote_copy(
            src_ref=src,
            dst_ref=dst,
            send_sem=send_sem,
            recv_sem=recv_sem,
            device_id=peer,
            device_id_type=MESH,
        )
        copy.start()
        return copy

    relayed = side == 8
    near, far, across, own = {}, {}, {}, {}
    for k in range(1, side):
        for i in range(count):
            peers = y_peers if i == 0 else z_peers
            near[i, k] = send(
                ins[i], outs[i].at[z, y, core], near_send.at[i, k], near_recv.at[i, k], peers[k]
            )
    for i in range(count):
        own[i] = pltpu.make_async_copy(ins[i], outs[i].at[z, y, core], own_sem.at[i])
        own[i].start()
    if works:
        works[0](given, made, scratch)
    for i in range(count):
        own[i].wait()
        for k in range(1, side):
            near[i, k].wait()
        peers = z_peers if i == 0 else y_peers
        for k in range(1, side):
            if relayed and 2 < k < side - 2:
                continue
            far[i, k] = send(
                slab(i, 0), slab(i, 0), far_send.at[i, k], far_recv.at[i, k], peers[k]
            )
        across[i, 0] = send(
            slab(i, 0), slab(i, 0), core_send.at[i, 0], core_recv.at[i, 0], partner
        )
    if works:
        works[1](given, made, scratch)
    half = side // 2
    order = [1, side - 1, 2, side - 2, 3, side - 3, half] if relayed else range(1, side)
    for k in order:
        for i in range(count):
            peers = z_peers if i == 0 else y_peers
            far[i, k].wait()
            if relayed and k == half:
                far[i, 0].wait()
            if relayed and k in (2, side - 2):
                to, number, start = (1, half, 0) if k == 2 else (side - 1, 0, half)
                far[i, 3 if k == 2 else side - 3] = send(
                    slab(i, k),
                    slab(i, k),
                    far_send.at[i, 3 if k == 2 else side - 3],
                    far_recv.at[i, 3 if k == 2 else side - 3],
                    peers[to],
                )
                far[i, number] = send(
                    slab(i, k, start, half),
                    slab(i, k, start, half),
                    far_send.at[i, number],
                    far_recv.at[i, number],
                    peers[k],
                )
            across[i, k] = send(
                slab(i, k), slab(i, k), core_send.at[i, k], core_recv.at[i, k], partner
            )
    for k in range(side):
        for i in range(count):
            across[i, k].wait()


def gather_blocks(first, second, collective_id, given=(), made=(), scratch=(), works=None):
    shard_count = lax.axis_size("shard")
    side = math.isqrt(shard_count // 2)
    sems = pltpu.SemaphoreType.DMA((2, side))
    outs = pl.pallas_call(
        functools.partial(gather_kernel, side, 2, len(given), len(made), works),
        out_shape=[
            jax.ShapeDtypeStruct((side, side, 2) + b.shape, b.dtype) for b in (first, second)
        ]
        + list(made),
        in_specs=[pl.BlockSpec(memory_space=pltpu.VMEM)] * (2 + len(given)),
        out_specs=[pl.BlockSpec(memory_space=pltpu.VMEM)] * (2 + len(made)),
        scratch_shapes=[pltpu.SemaphoreType.DMA((2,))] + [sems] * 6 + list(scratch),
        compiler_params=pltpu.CompilerParams(
            collective_id=collective_id, has_side_effects=True, vmem_limit_bytes=48 * 2**20
        ),
    )(first, second, *given)
    return [o.reshape((shard_count,) + o.shape[3:]) for o in outs[:2]] + list(outs[2:])


def prerank_work(given, made, scratch):
    attributes, inner, offset, grading = given[:4]
    (scores,) = scratch

    def step(t, carry):
        block = attributes[pl.ds(pl.multiple_of(t * LANES, LANES), LANES), :]
        hidden = jnp.maximum(fdot(block, inner[...]) + offset[...], 0.0).astype(BF16)
        scores[t] = lax.dot_general(
            grading[...], hidden, (((1,), (1,)), ((), ())), preferred_element_type=F32
        )
        return carry

    lax.fori_loop(0, attributes.shape[0] // LANES, step, 0)


def gate_work(rounds, given, made, scratch):
    positions, keep, rows, pick = given[4:]
    gates, gated = made
    (scores,) = scratch
    entries = rows.shape[0] // rounds
    steps = scores.shape[0] // rounds
    span = pick.shape[0]
    for r in range(rounds):
        here = pl.ds(r * entries, entries)
        looked_up = jnp.zeros((entries, LANES), F32)
        for t in range(steps):
            ids = lax.broadcasted_iota(jnp.int32, (entries, LANES), 1) + t * LANES
            row = scores[r * steps + t][0:1, :]
            looked_up += jnp.where(positions[here, :] == ids, row, 0.0)
        score = jnp.sum(looked_up, axis=1, keepdims=True)
        small = jnp.exp(-jnp.abs(score))
        gate = keep[here, :] * jnp.where(score >= 0.0, 1.0, small) / (1.0 + small)
        gates[here, :] = gate
        for g in range(rows.shape[1] // span):
            part = fdot(rows[here, g * span : (g + 1) * span], pick[...])
            gated[here, g * LANES : (g + 1) * LANES] = (part * gate).astype(BF16)


NT = (((1,), (1,)), ((), ()))


def section_kernel(
    count,
    h0,
    keep,
    keep_row,
    owner,
    gain,
    wide,
    lower1,
    lower2,
    lower3,
    raise1,
    raise2,
    raise3,
    out_ref,
    x_ref,
    out1_ref,
    slots1,
    slots2,
    part3,
    slots3,
    slots4,
    send_sem,
    recv_sem,
):
    segment = lax.axis_index("segment")
    me = lax.axis_index("shard")
    rows, width = x_ref.shape
    low_rank = lower1.shape[1]
    owners = gain.shape[0] * LANES // width
    per = width // LANES
    peers = [(lax.rem(segment + k, count), me) for k in range(1, count)]
    barrier = pltpu.get_barrier_semaphore()
    for peer in peers:
        pl.semaphore_signal(barrier, inc=1, device_id=peer, device_id_type=MESH)

    def exchange(number, slots):
        copies = []
        for k, peer in enumerate(peers):
            copies.append(
                pltpu.make_async_remote_copy(
                    src_ref=slots.at[segment],
                    dst_ref=slots.at[segment],
                    send_sem=send_sem.at[number, k],
                    recv_sem=recv_sem.at[number, k],
                    device_id=peer,
                    device_id_type=MESH,
                )
            )
            copies[-1].start()
        return copies

    def total(slots, start, size):
        value = slots[0, start : start + size]
        for k in range(1, count):
            value = value + slots[k, start : start + size]
        return value

    owner_hot = (
        owner[...] == lax.broadcasted_iota(jnp.int32, (rows, owners), 1)
    ).astype(F32).astype(BF16)
    for g in range(per):
        gain_g = gain[pl.ds(g, owners, stride=per), :].astype(BF16)
        lanes = slice(g * LANES, (g + 1) * LANES)
        x_ref[:, lanes] = (h0[:, lanes].astype(F32) * fdot(owner_hot, gain_g)).astype(BF16)
    slots1[segment] = fdot(x_ref[...], lower1[...])
    pl.semaphore_wait(barrier, count - 1)
    first = exchange(0, slots1)

    table = wide[...]
    slots2[segment, 0:low_rank] = lax.dot_general(
        raise2[...], lower3[...], (((0,), (0,)), ((), ())), preferred_element_type=F32
    )
    for n, matrix in enumerate((raise2, raise3, lower3)):
        at = low_rank + 8 * n
        slots2[segment, at : at + 8] = fdot(table, matrix[...].astype(F32), HIGH)
    consts = [
        jnp.sum(table[a : a + 1] * table[b : b + 1], axis=1, keepdims=True)
        for a, b in ((1, 4), (1, 5), (2, 5))
    ]
    row = lax.broadcasted_iota(jnp.int32, (8, low_rank), 0)
    slots2[segment, low_rank + 24 : low_rank + 32] = jnp.where(
        row == 0, consts[0], jnp.where(row == 1, consts[1], consts[2])
    )
    for copy in first:
        copy.wait()
    weights = exchange(1, slots2)

    act1 = total(slots1, 0, rows).astype(BF16)
    for g in range(per):
        lanes = slice(g * LANES, (g + 1) * LANES)
        lifted = (
            lax.dot_general(act1, raise1[lanes, :], NT, preferred_element_type=F32)
            + table[0:1, lanes]
        )
        x32 = x_ref[:, lanes].astype(F32)
        out1 = (x32 + x32 * lifted) * keep[...]
        out1_ref[:, lanes] = out1
        x_ref[:, lanes] = out1.astype(BF16)
    h1 = x_ref[...]
    quarter = rows // count
    for n, matrix in enumerate((lower2, lower3)):
        product = fdot(h1, matrix[...])
        for k in range(count):
            part3[k, n * quarter : (n + 1) * quarter] = product[k * quarter : (k + 1) * quarter]
    graded1 = lax.dot_general(table, out1_ref[...], NT, precision=HIGH, preferred_element_type=F32)
    graded = lax.dot_general(
        table, h1.astype(F32), NT, precision=HIGH, preferred_element_type=F32
    )
    which = lax.broadcasted_iota(jnp.int32, graded.shape, 0)
    graded = jnp.where(which == 3, graded1, graded)
    for c in range(rows // LANES):
        at = 2 * quarter + 8 * c
        for k in range(count):
            part3[k, at : at + 8] = graded[:, c * LANES : (c + 1) * LANES]
    slots3[segment] = part3[segment]
    for copy in weights:
        copy.wait()
    between = total(slots2, 0, low_rank)
    raised2 = total(slots2, low_rank, 8)
    raised3 = total(slots2, low_rank + 8, 8)
    lowered = total(slots2, low_rank + 16, 8)
    consts = total(slots2, low_rank + 24, 8)
    copies = []
    for k, peer in enumerate(peers):
        copies.append(
            pltpu.make_async_remote_copy(
                src_ref=part3.at[peer[0]],
                dst_ref=slots3.at[segment],
                send_sem=send_sem.at[2, k],
                recv_sem=recv_sem.at[2, k],
                device_id=peer,
                device_id_type=MESH,
            )
        )
        copies[-1].start()
    for copy in copies:
        copy.wait()

    begin = pl.multiple_of(segment * quarter, quarter)
    act2 = jnp.maximum(total(slots3, 0, quarter), 0.0).astype(BF16).astype(F32)
    inner3 = (
        total(slots3, quarter, quarter) + fdot(act2, between, HIGH) + lowered[1:2]
    ) * keep[pl.ds(begin, quarter), :]
    act3 = jnp.maximum(inner3, 0.0).astype(BF16).astype(F32)
    act2 = jnp.concatenate([act2] * count, 0)
    act3 = jnp.concatenate([act3] * count, 0)
    from2 = lax.dot_general(raised2, act2, NT, precision=HIGH, preferred_element_type=F32)
    from3 = lax.dot_general(raised3, act3, NT, precision=HIGH, preferred_element_type=F32)
    row = lax.broadcasted_iota(jnp.int32, (8, LANES), 0)
    lane = lax.broadcasted_iota(jnp.int32, (8, LANES), 1)
    for c in range(rows // LANES):
        lanes = slice(c * LANES, (c + 1) * LANES)
        graded = total(slots3, 2 * quarter + 8 * c, 8)
        kept = keep_row[0:1, lanes]
        second = (graded[4:5] + from2[4:5, lanes] + consts[0:1]) * kept
        third = (
            (graded[5:6] + from2[5:6, lanes] + consts[1:2]) * kept
            + from3[5:6, lanes]
            + consts[2:3]
        ) * kept
        value = jnp.where(row == 0, graded[3:4], jnp.where(row == 1, second, third))
        mine = (lane + c * LANES >= begin) & (lane + c * LANES < begin + quarter)
        slots4[segment, 8 * c : 8 * c + 8] = jnp.where(mine, value, 0.0)
    for copy in exchange(3, slots4):
        copy.wait()
    for c in range(rows // LANES):
        out_ref[:, c * LANES : (c + 1) * LANES] = total(slots4, 8 * c, 8)[0:3]


def run_sections(collective_id, *operands):
    count = lax.axis_size("segment")
    rows, width = operands[0].shape
    low_rank = operands[6].shape[1]
    sems = pltpu.SemaphoreType.DMA((4, count - 1))
    return pl.pallas_call(
        functools.partial(section_kernel, count),
        out_shape=jax.ShapeDtypeStruct((3, rows), F32),
        in_specs=[pl.BlockSpec(memory_space=pltpu.VMEM)] * len(operands),
        out_specs=pl.BlockSpec(memory_space=pltpu.VMEM),
        scratch_shapes=[
            pltpu.VMEM((rows, width), BF16),
            pltpu.VMEM((rows, width), F32),
            pltpu.VMEM((count, rows, low_rank), F32),
            pltpu.VMEM((count, low_rank + 32, low_rank), F32),
            pltpu.VMEM((count, 2 * rows // count + rows // LANES * 8, low_rank), F32),
            pltpu.VMEM((count, 2 * rows // count + rows // LANES * 8, low_rank), F32),
            pltpu.VMEM((count, rows // LANES * 8, low_rank), F32),
            sems,
            sems,
        ],
        compiler_params=pltpu.CompilerParams(
            collective_id=collective_id, has_side_effects=True, vmem_limit_bytes=48 * 2**20
        ),
    )(*operands)


def local(
    proposal_attributes,
    keeper_ordering_vectors,
    keeper_positions,
    alive_tallies,
    holder_shards,
    holder_attribute_factor,
    early_inner_matrix,
    early_inner_offset,
    early_grading_vector,
    block_lowering_matrices,
    block_raising_flipped,
    block_result_offsets,
    block_grading_vectors,
):
    segment_id = lax.axis_index("segment")
    segment_count = lax.axis_size("segment")
    shard_count = lax.axis_size("shard")
    rounds, entries, width = keeper_ordering_vectors.shape
    candidates = proposal_attributes.shape[1]
    low_rank = block_lowering_matrices.shape[2]
    cap_slots = max(2, 2 * entries // shard_count)
    rows = rounds * entries
    own_features = width // shard_count
    piece = own_features // segment_count
    part_width = width // segment_count
    span = segment_count * LANES
    spans = width // span

    at = lax.broadcasted_iota(jnp.int32, (span, LANES), 0)
    to = lax.broadcasted_iota(jnp.int32, (span, LANES), 1)
    chosen = (at // own_features == to // piece) & (
        at % own_features == segment_id * piece + to % piece
    )
    pick = chosen.astype(BF16)
    pick32 = chosen.astype(F32)

    wide = jnp.concatenate(
        [holder_attribute_factor.astype(F32), block_result_offsets, block_grading_vectors], 0
    )
    wide = fdot(wide.reshape(7 * spans, span), pick32, HIGH)
    own_gain = wide[:spans].astype(BF16)
    wide = wide[spans:].reshape(6, part_width)
    own_lower = lax.dynamic_slice_in_dim(block_lowering_matrices, segment_id * piece, piece, 1)
    own_raise = lax.dynamic_slice_in_dim(block_raising_flipped, segment_id * piece, piece, 1)
    owner = holder_shards[:, :, 0]
    keep = (keeper_positions < alive_tallies).astype(F32)
    keep_col = keep.reshape(rows, 1)
    lower_blocks, raise_blocks, gate_col, h0 = gather_blocks(
        own_lower.reshape(3 * piece, low_rank),
        jnp.concatenate([own_raise.reshape(3 * piece, low_rank), own_gain], 0),
        0,
        (
            proposal_attributes.reshape(rounds * candidates, -1),
            early_inner_matrix,
            early_inner_offset[None],
            jnp.broadcast_to(early_grading_vector, (8,) + early_grading_vector.shape),
            keeper_positions.reshape(rows, 1),
            keep_col,
            keeper_ordering_vectors.reshape(rows, width),
            pick,
        ),
        (
            jax.ShapeDtypeStruct((rows, 1), F32),
            jax.ShapeDtypeStruct((rows, part_width), BF16),
        ),
        (pltpu.VMEM((rounds * candidates // LANES, 8, LANES), F32),),
        (prerank_work, functools.partial(gate_work, rounds)),
    )

    def matrix(blocks, k):
        return blocks[:, k * piece : (k + 1) * piece].reshape(part_width, low_rank)

    order = jnp.arange(entries, dtype=jnp.int32)
    same = (owner[:, :, None] == owner[:, None, :]) & (order[None, :] < order[:, None])
    within = jnp.sum(same.astype(jnp.int32), axis=2)
    owners = jnp.arange(shard_count, dtype=jnp.int32)
    places = jnp.arange(cap_slots, dtype=jnp.int32)
    placed = (owner[:, None, None, :] == owners[:, None]) & (
        within[:, None, None, :] == places[:, None, None]
    )

    gain = raise_blocks[:, 3 * piece :].astype(F32).reshape(-1, LANES)
    graded = run_sections(
        1,
        h0,
        keep_col,
        keep.reshape(1, rows),
        owner.reshape(rows, 1),
        gain,
        jnp.pad(wide, ((0, 2), (0, 0))),
        *[matrix(lower_blocks, k) for k in range(3)],
        *[matrix(raise_blocks, k) for k in range(3)],
    )
    section = jnp.concatenate([gate_col.reshape(1, rows), graded], 0)
    values = lax.dynamic_index_in_dim(section, segment_id, 0, keepdims=False)
    values = values.reshape(rounds, 1, 1, entries)
    sent = jnp.sum(jnp.where(placed, values, 0.0), axis=3)
    boards = jnp.stack(gather_blocks(sent[0], sent[1], 3))
    mine = owners == lax.axis_index("shard")
    arrived = jnp.sum(jnp.where(mine, boards, 0.0), axis=3)
    result = jnp.where(segment_id == 0, sent.transpose(0, 2, 1), arrived)
    return result.reshape(1, rounds, shard_count * cap_slots)


def solution(mesh):
    placed = (
        P(None, "shard", None),
        P(None, "shard", None),
        P(None, "shard"),
        P(None, "shard"),
        P(None, "shard", None),
        P("shard", None),
        P(),
        P(),
        P(),
        P(None, "shard", None),
        P(None, "shard", None),
        P(),
        P(),
    )
    return jax.shard_map(
        local, mesh=mesh, in_specs=placed, out_specs=P("segment", None, "shard"), check_vma=False
    )
```

```python
import functools
import math

import jax
import jax.numpy as jnp
from jax import lax
from jax.experimental import pallas as pl
from jax.experimental.pallas import tpu as pltpu
from jax.sharding import PartitionSpec as P

F32 = jnp.float32
BF16 = jnp.bfloat16
HIGH = lax.Precision.HIGHEST
LANES = 128


def fdot(a, b, precision=None):
    return jnp.dot(a, b, preferred_element_type=F32, precision=precision)


MESH = pl.DeviceIdType.MESH


def gather_kernel(side, count, extra_in, extra_out, works, *refs):
    ins, given = refs[:count], refs[count : count + extra_in]
    refs = refs[count + extra_in :]
    outs, made = refs[:count], refs[count : count + extra_out]
    refs = refs[count + extra_out :]
    own_sem, near_send, near_recv, far_send, far_recv, core_send, core_recv = refs[:7]
    scratch = refs[7:]
    segment = lax.axis_index("segment")
    me = lax.axis_index("shard")
    core = lax.rem(me, 2)
    y = lax.rem(me // 2, side)
    z = me // (2 * side)

    def device(zz, yy, cc):
        return (segment, (zz * side + yy) * 2 + cc)

    def turned(value, by):
        return lax.rem(value + by + side, side)

    y_peers = [None] + [device(z, turned(y, k), core) for k in range(1, side)]
    z_peers = [None] + [device(turned(z, k), y, core) for k in range(1, side)]
    partner = device(z, y, 1 - core)

    barrier = pltpu.get_barrier_semaphore()
    for peer in y_peers[1:] + z_peers[1:] + [partner]:
        pl.semaphore_signal(barrier, inc=1, device_id=peer, device_id_type=MESH)
    pl.semaphore_wait(barrier, 2 * side - 1)

    def slab(i, k, start=0, size=side):
        if i == 0:
            return outs[i].at[turned(z, -k), pl.ds(start, size), core]
        return outs[i].at[pl.ds(start, size), turned(y, -k), core]

    def send(src, dst, send_sem, recv_sem, peer):
        copy = pltpu.make_async_remote_copy(
            src_ref=src,
            dst_ref=dst,
            send_sem=send_sem,
            recv_sem=recv_sem,
            device_id=peer,
            device_id_type=MESH,
        )
        copy.start()
        return copy

    relayed = side == 8 and bool(works)
    near, far, across, own = {}, {}, {}, {}
    for k in range(1, side):
        for i in range(count):
            peers = y_peers if i == 0 else z_peers
            near[i, k] = send(
                ins[i], outs[i].at[z, y, core], near_send.at[i, k], near_recv.at[i, k], peers[k]
            )
    for i in range(count):
        own[i] = pltpu.make_async_copy(ins[i], outs[i].at[z, y, core], own_sem.at[i])
        own[i].start()
    if works:
        works[0](given, made, scratch)
    for i in range(count):
        own[i].wait()
        for k in range(1, side):
            near[i, k].wait()
        peers = z_peers if i == 0 else y_peers
        for k in range(1, side):
            if relayed and 2 < k < side - 2:
                continue
            far[i, k] = send(
                slab(i, 0), slab(i, 0), far_send.at[i, k], far_recv.at[i, k], peers[k]
            )
        across[i, 0] = send(
            slab(i, 0), slab(i, 0), core_send.at[i, 0], core_recv.at[i, 0], partner
        )
    if works:
        works[1](given, made, scratch)
    half = side // 2
    order = [1, side - 1, 2, side - 2, 3, side - 3, half] if relayed else range(1, side)
    for k in order:
        for i in range(count):
            peers = z_peers if i == 0 else y_peers
            far[i, k].wait()
            if relayed and k == half:
                far[i, 0].wait()
            if relayed and k in (2, side - 2):
                to, number, start = (1, half, 0) if k == 2 else (side - 1, 0, half)
                far[i, 3 if k == 2 else side - 3] = send(
                    slab(i, k),
                    slab(i, k),
                    far_send.at[i, 3 if k == 2 else side - 3],
                    far_recv.at[i, 3 if k == 2 else side - 3],
                    peers[to],
                )
                far[i, number] = send(
                    slab(i, k, start, half),
                    slab(i, k, start, half),
                    far_send.at[i, number],
                    far_recv.at[i, number],
                    peers[k],
                )
            across[i, k] = send(
                slab(i, k), slab(i, k), core_send.at[i, k], core_recv.at[i, k], partner
            )
    for k in range(side):
        for i in range(count):
            across[i, k].wait()


def gather_blocks(first, second, collective_id, given=(), made=(), scratch=(), works=None):
    shard_count = lax.axis_size("shard")
    side = math.isqrt(shard_count // 2)
    sems = pltpu.SemaphoreType.DMA((2, side))
    outs = pl.pallas_call(
        functools.partial(gather_kernel, side, 2, len(given), len(made), works),
        out_shape=[
            jax.ShapeDtypeStruct((side, side, 2) + b.shape, b.dtype) for b in (first, second)
        ]
        + list(made),
        in_specs=[pl.BlockSpec(memory_space=pltpu.VMEM)] * (2 + len(given)),
        out_specs=[pl.BlockSpec(memory_space=pltpu.VMEM)] * (2 + len(made)),
        scratch_shapes=[pltpu.SemaphoreType.DMA((2,))] + [sems] * 6 + list(scratch),
        compiler_params=pltpu.CompilerParams(
            collective_id=collective_id, has_side_effects=True, vmem_limit_bytes=48 * 2**20
        ),
    )(first, second, *given)
    return [o.reshape((shard_count,) + o.shape[3:]) for o in outs[:2]] + list(outs[2:])


def prerank_work(given, made, scratch):
    attributes, inner, offset, grading = given[:4]
    (scores,) = scratch

    def step(t, carry):
        block = attributes[pl.ds(pl.multiple_of(t * LANES, LANES), LANES), :]
        hidden = jnp.maximum(fdot(block, inner[...]) + offset[...], 0.0).astype(BF16)
        scores[t] = lax.dot_general(
            grading[...], hidden, (((1,), (1,)), ((), ())), preferred_element_type=F32
        )
        return carry

    lax.fori_loop(0, attributes.shape[0] // LANES, step, 0)


def gate_work(rounds, given, made, scratch):
    positions, keep, rows, pick = given[4:]
    gates, gated = made
    (scores,) = scratch
    entries = rows.shape[0] // rounds
    steps = scores.shape[0] // rounds
    span = pick.shape[0]
    for r in range(rounds):
        here = pl.ds(r * entries, entries)
        looked_up = jnp.zeros((entries, LANES), F32)
        for t in range(steps):
            ids = lax.broadcasted_iota(jnp.int32, (entries, LANES), 1) + t * LANES
            row = scores[r * steps + t][0:1, :]
            looked_up += jnp.where(positions[here, :] == ids, row, 0.0)
        score = jnp.sum(looked_up, axis=1, keepdims=True)
        small = jnp.exp(-jnp.abs(score))
        gate = keep[here, :] * jnp.where(score >= 0.0, 1.0, small) / (1.0 + small)
        gates[here, :] = gate
        for g in range(rows.shape[1] // span):
            part = fdot(rows[here, g * span : (g + 1) * span], pick[...])
            gated[here, g * LANES : (g + 1) * LANES] = (part * gate).astype(BF16)


NT = (((1,), (1,)), ((), ()))


def section_kernel(
    count,
    h0,
    keep,
    keep_row,
    owner,
    gain,
    wide,
    lower1,
    lower2,
    lower3,
    raise1,
    raise2,
    raise3,
    out_ref,
    x_ref,
    out1_ref,
    slots1,
    slots2,
    part3,
    slots3,
    slots4,
    send_sem,
    recv_sem,
):
    segment = lax.axis_index("segment")
    me = lax.axis_index("shard")
    rows, width = x_ref.shape
    low_rank = lower1.shape[1]
    owners = gain.shape[0] * LANES // width
    per = width // LANES
    peers = [(lax.rem(segment + k, count), me) for k in range(1, count)]
    barrier = pltpu.get_barrier_semaphore()
    for peer in peers:
        pl.semaphore_signal(barrier, inc=1, device_id=peer, device_id_type=MESH)

    def exchange(number, slots):
        copies = []
        for k, peer in enumerate(peers):
            copies.append(
                pltpu.make_async_remote_copy(
                    src_ref=slots.at[segment],
                    dst_ref=slots.at[segment],
                    send_sem=send_sem.at[number, k],
                    recv_sem=recv_sem.at[number, k],
                    device_id=peer,
                    device_id_type=MESH,
                )
            )
            copies[-1].start()
        return copies

    def total(slots, start, size):
        value = slots[0, start : start + size]
        for k in range(1, count):
            value = value + slots[k, start : start + size]
        return value

    owner_hot = (
        owner[...] == lax.broadcasted_iota(jnp.int32, (rows, owners), 1)
    ).astype(F32).astype(BF16)
    for g in range(per):
        gain_g = gain[pl.ds(g, owners, stride=per), :].astype(BF16)
        lanes = slice(g * LANES, (g + 1) * LANES)
        x_ref[:, lanes] = (h0[:, lanes].astype(F32) * fdot(owner_hot, gain_g)).astype(BF16)
    slots1[segment] = fdot(x_ref[...], lower1[...])
    pl.semaphore_wait(barrier, count - 1)
    first = exchange(0, slots1)

    table = wide[...]
    slots2[segment, 0:low_rank] = lax.dot_general(
        raise2[...], lower3[...], (((0,), (0,)), ((), ())), preferred_element_type=F32
    )
    for n, matrix in enumerate((raise2, raise3, lower3)):
        at = low_rank + 8 * n
        slots2[segment, at : at + 8] = fdot(table, matrix[...].astype(F32), HIGH)
    consts = [
        jnp.sum(table[a : a + 1] * table[b : b + 1], axis=1, keepdims=True)
        for a, b in ((1, 4), (1, 5), (2, 5))
    ]
    row = lax.broadcasted_iota(jnp.int32, (8, low_rank), 0)
    slots2[segment, low_rank + 24 : low_rank + 32] = jnp.where(
        row == 0, consts[0], jnp.where(row == 1, consts[1], consts[2])
    )
    for copy in first:
        copy.wait()
    weights = exchange(1, slots2)

    act1 = total(slots1, 0, rows).astype(BF16)
    for g in range(per):
        lanes = slice(g * LANES, (g + 1) * LANES)
        lifted = (
            lax.dot_general(act1, raise1[lanes, :], NT, preferred_element_type=F32)
            + table[0:1, lanes]
        )
        x32 = x_ref[:, lanes].astype(F32)
        out1 = (x32 + x32 * lifted) * keep[...]
        out1_ref[:, lanes] = out1
        x_ref[:, lanes] = out1.astype(BF16)
    h1 = x_ref[...]
    quarter = rows // count
    for n, matrix in enumerate((lower2, lower3)):
        product = fdot(h1, matrix[...])
        for k in range(count):
            part3[k, n * quarter : (n + 1) * quarter] = product[k * quarter : (k + 1) * quarter]
    graded1 = lax.dot_general(table, out1_ref[...], NT, precision=HIGH, preferred_element_type=F32)
    graded = lax.dot_general(
        table, h1.astype(F32), NT, precision=HIGH, preferred_element_type=F32
    )
    which = lax.broadcasted_iota(jnp.int32, graded.shape, 0)
    graded = jnp.where(which == 3, graded1, graded)
    for c in range(rows // LANES):
        at = 2 * quarter + 8 * c
        for k in range(count):
            part3[k, at : at + 8] = graded[:, c * LANES : (c + 1) * LANES]
    slots3[segment] = part3[segment]
    for copy in weights:
        copy.wait()
    between = total(slots2, 0, low_rank)
    raised2 = total(slots2, low_rank, 8)
    raised3 = total(slots2, low_rank + 8, 8)
    lowered = total(slots2, low_rank + 16, 8)
    consts = total(slots2, low_rank + 24, 8)
    copies = []
    for k, peer in enumerate(peers):
        copies.append(
            pltpu.make_async_remote_copy(
                src_ref=part3.at[peer[0]],
                dst_ref=slots3.at[segment],
                send_sem=send_sem.at[2, k],
                recv_sem=recv_sem.at[2, k],
                device_id=peer,
                device_id_type=MESH,
            )
        )
        copies[-1].start()
    for copy in copies:
        copy.wait()

    begin = pl.multiple_of(segment * quarter, quarter)
    act2 = jnp.maximum(total(slots3, 0, quarter), 0.0).astype(BF16).astype(F32)
    inner3 = (
        total(slots3, quarter, quarter) + fdot(act2, between, HIGH) + lowered[1:2]
    ) * keep[pl.ds(begin, quarter), :]
    act3 = jnp.maximum(inner3, 0.0).astype(BF16).astype(F32)
    act2 = jnp.concatenate([act2] * count, 0)
    act3 = jnp.concatenate([act3] * count, 0)
    from2 = lax.dot_general(raised2, act2, NT, precision=HIGH, preferred_element_type=F32)
    from3 = lax.dot_general(raised3, act3, NT, precision=HIGH, preferred_element_type=F32)
    row = lax.broadcasted_iota(jnp.int32, (8, LANES), 0)
    lane = lax.broadcasted_iota(jnp.int32, (8, LANES), 1)
    for c in range(rows // LANES):
        lanes = slice(c * LANES, (c + 1) * LANES)
        graded = total(slots3, 2 * quarter + 8 * c, 8)
        kept = keep_row[0:1, lanes]
        second = (graded[4:5] + from2[4:5, lanes] + consts[0:1]) * kept
        third = (
            (graded[5:6] + from2[5:6, lanes] + consts[1:2]) * kept
            + from3[5:6, lanes]
            + consts[2:3]
        ) * kept
        value = jnp.where(row == 0, graded[3:4], jnp.where(row == 1, second, third))
        mine = (lane + c * LANES >= begin) & (lane + c * LANES < begin + quarter)
        slots4[segment, 8 * c : 8 * c + 8] = jnp.where(mine, value, 0.0)
    for copy in exchange(3, slots4):
        copy.wait()
    for c in range(rows // LANES):
        out_ref[:, c * LANES : (c + 1) * LANES] = total(slots4, 8 * c, 8)[0:3]


def run_sections(collective_id, *operands):
    count = lax.axis_size("segment")
    rows, width = operands[0].shape
    low_rank = operands[6].shape[1]
    sems = pltpu.SemaphoreType.DMA((4, count - 1))
    return pl.pallas_call(
        functools.partial(section_kernel, count),
        out_shape=jax.ShapeDtypeStruct((3, rows), F32),
        in_specs=[pl.BlockSpec(memory_space=pltpu.VMEM)] * len(operands),
        out_specs=pl.BlockSpec(memory_space=pltpu.VMEM),
        scratch_shapes=[
            pltpu.VMEM((rows, width), BF16),
            pltpu.VMEM((rows, width), F32),
            pltpu.VMEM((count, rows, low_rank), F32),
            pltpu.VMEM((count, low_rank + 32, low_rank), F32),
            pltpu.VMEM((count, 2 * rows // count + rows // LANES * 8, low_rank), F32),
            pltpu.VMEM((count, 2 * rows // count + rows // LANES * 8, low_rank), F32),
            pltpu.VMEM((count, rows // LANES * 8, low_rank), F32),
            sems,
            sems,
        ],
        compiler_params=pltpu.CompilerParams(
            collective_id=collective_id, has_side_effects=True, vmem_limit_bytes=48 * 2**20
        ),
    )(*operands)


def local(
    proposal_attributes,
    keeper_ordering_vectors,
    keeper_positions,
    alive_tallies,
    holder_shards,
    holder_attribute_factor,
    early_inner_matrix,
    early_inner_offset,
    early_grading_vector,
    block_lowering_matrices,
    block_raising_flipped,
    block_result_offsets,
    block_grading_vectors,
):
    segment_id = lax.axis_index("segment")
    segment_count = lax.axis_size("segment")
    shard_count = lax.axis_size("shard")
    rounds, entries, width = keeper_ordering_vectors.shape
    candidates = proposal_attributes.shape[1]
    low_rank = block_lowering_matrices.shape[2]
    cap_slots = max(2, 2 * entries // shard_count)
    rows = rounds * entries
    own_features = width // shard_count
    piece = own_features // segment_count
    part_width = width // segment_count
    span = segment_count * LANES
    spans = width // span

    at = lax.broadcasted_iota(jnp.int32, (span, LANES), 0)
    to = lax.broadcasted_iota(jnp.int32, (span, LANES), 1)
    chosen = (at // own_features == to // piece) & (
        at % own_features == segment_id * piece + to % piece
    )
    pick = chosen.astype(BF16)
    pick32 = chosen.astype(F32)

    wide = jnp.concatenate(
        [holder_attribute_factor.astype(F32), block_result_offsets, block_grading_vectors], 0
    )
    wide = fdot(wide.reshape(7 * spans, span), pick32, HIGH)
    own_gain = wide[:spans].astype(BF16)
    wide = wide[spans:].reshape(6, part_width)
    own_lower = lax.dynamic_slice_in_dim(block_lowering_matrices, segment_id * piece, piece, 1)
    own_raise = lax.dynamic_slice_in_dim(block_raising_flipped, segment_id * piece, piece, 1)
    owner = holder_shards[:, :, 0]
    keep = (keeper_positions < alive_tallies).astype(F32)
    keep_col = keep.reshape(rows, 1)
    lower_blocks, raise_blocks, gate_col, h0 = gather_blocks(
        own_lower.reshape(3 * piece, low_rank),
        jnp.concatenate([own_raise.reshape(3 * piece, low_rank), own_gain], 0),
        0,
        (
            proposal_attributes.reshape(rounds * candidates, -1),
            early_inner_matrix,
            early_inner_offset[None],
            jnp.broadcast_to(early_grading_vector, (8,) + early_grading_vector.shape),
            keeper_positions.reshape(rows, 1),
            keep_col,
            keeper_ordering_vectors.reshape(rows, width),
            pick,
        ),
        (
            jax.ShapeDtypeStruct((rows, 1), F32),
            jax.ShapeDtypeStruct((rows, part_width), BF16),
        ),
        (pltpu.VMEM((rounds * candidates // LANES, 8, LANES), F32),),
        (prerank_work, functools.partial(gate_work, rounds)),
    )

    def matrix(blocks, k):
        return blocks[:, k * piece : (k + 1) * piece].reshape(part_width, low_rank)

    order = jnp.arange(entries, dtype=jnp.int32)
    same = (owner[:, :, None] == owner[:, None, :]) & (order[None, :] < order[:, None])
    within = jnp.sum(same.astype(jnp.int32), axis=2)
    owners = jnp.arange(shard_count, dtype=jnp.int32)
    places = jnp.arange(cap_slots, dtype=jnp.int32)
    placed = (owner[:, None, None, :] == owners[:, None]) & (
        within[:, None, None, :] == places[:, None, None]
    )

    gain = raise_blocks[:, 3 * piece :].astype(F32).reshape(-1, LANES)
    graded = run_sections(
        1,
        h0,
        keep_col,
        keep.reshape(1, rows),
        owner.reshape(rows, 1),
        gain,
        jnp.pad(wide, ((0, 2), (0, 0))),
        *[matrix(lower_blocks, k) for k in range(3)],
        *[matrix(raise_blocks, k) for k in range(3)],
    )
    section = jnp.concatenate([gate_col.reshape(1, rows), graded], 0)
    values = lax.dynamic_index_in_dim(section, segment_id, 0, keepdims=False)
    values = values.reshape(rounds, 1, 1, entries)
    sent = jnp.sum(jnp.where(placed, values, 0.0), axis=3)
    boards = jnp.stack(gather_blocks(sent[0], sent[1], 3))
    mine = owners == lax.axis_index("shard")
    arrived = jnp.sum(jnp.where(mine, boards, 0.0), axis=3)
    result = jnp.where(segment_id == 0, sent.transpose(0, 2, 1), arrived)
    return result.reshape(1, rounds, shard_count * cap_slots)


def solution(mesh):
    placed = (
        P(None, "shard", None),
        P(None, "shard", None),
        P(None, "shard"),
        P(None, "shard"),
        P(None, "shard", None),
        P("shard", None),
        P(),
        P(),
        P(),
        P(None, "shard", None),
        P(None, "shard", None),
        P(),
        P(),
    )
    return jax.shard_map(
        local, mesh=mesh, in_specs=placed, out_specs=P("segment", None, "shard"), check_vma=False
    )
```
